32 devices in a mesh: dp: 4 (over y, x), rows: 8 (over z, core).
Axes of the slice: x: 2, y: 2, z: 4, core: 2. Of those that a mesh axis runs over, the one named last changes fastest.
Arguments:
- grad_out: bfloat16 [2048, 4096], P('dp', 'rows'), may hold values from -0.375 to 0.375
- activations: bfloat16 [2048, 4096], P('dp', 'rows'), may hold values from -6 to 6
- error_feedback: float32 [4, 4096, 4096], P('dp', 'rows'), may hold values from -6 to 6
- momentum: bfloat16 [4096, 4096], P('rows'), may hold values from -1.1953125 to 1.1953125
- right_factor: float32 [4096, 128], P('rows'), may hold values from -0.09375 to 0.09375
Outputs:
- new_error: float32 [4, 4096, 4096], P('dp', 'rows')
- new_momentum: bfloat16 [4096, 4096], P('rows')
- new_right: float32 [4096, 128], P('rows')
The draws below stay inside these ranges and needn't reach their ends.
All inputs are finite; a program needn't handle non-finite values.
Results may differ from the reference program's by a relative error of at most 0.0012.
Values may be sent and summed in bfloat16 or wider, within the bound.
No kernel may reach another device: no remote copies, remote signals or barrier semaphores. Data moves between devices by JAX's collectives and lax.ppermute only.
A program may use at most 64 MiB of HBM per device.

```python
import jax
import jax.numpy as jnp
from jax import lax

OUTPUTS = 4096
INPUTS = 4096
FACTOR_RANK = 128
PASSES = 2
TOK_DEV = 512
TOKENS = 2048
REPLICAS = 4
N_DP = 4


def shard_levels(own_key, shape, split, low, top_value):
    factor_of, own = 1.0, jax.random.fold_in(own_key, 6)
    for position, blocks in split:
        steps = jnp.exp(jax.random.uniform(jax.random.fold_in(own, position), (blocks,), jnp.float32, low / len(split), top_value / len(split)))
        factor_of = factor_of * jnp.repeat(steps, shape[position] // blocks).reshape([-1 if axis == position else 1 for axis in range(len(shape))])
    return factor_of


def centred(rng, extent, spread, limit, shards=(), kind=jnp.bfloat16):
    values = spread * jax.random.normal(rng, extent, jnp.float32)
    if shards:
        values = values * shard_levels(rng, extent, shards, -0.22, 0.18)
    return jnp.clip(values, -limit, limit).astype(kind)


def setup_inputs(seed: int = 0) -> dict:
    seeds = jax.random.split(jax.random.key(seed), 6)
    grad_out = centred(seeds[0], (TOKENS, OUTPUTS), 0.0625, 0.375, ((0, 4), (1, 8)))
    activations = centred(seeds[1], (TOKENS, INPUTS), 1.0, 6.0, ((0, 4), (1, 8)))
    error_feedback = centred(seeds[2], (REPLICAS, OUTPUTS, INPUTS), 1.0, 6.0, ((0, 4), (1, 8)), jnp.float32)
    momentum = centred(seeds[3], (OUTPUTS, INPUTS), 0.2, 1.1953125, ((0, 8),))
    right_factor = centred(seeds[4], (INPUTS, FACTOR_RANK), INPUTS ** -0.5, 0.09375, ((0, 8),), jnp.float32)
    return dict(grad_out=grad_out, activations=activations, error_feedback=error_feedback, momentum=momentum, right_factor=right_factor)


MOMENTUM_RATE = 0.9
HIGHEST = lax.Precision.HIGHEST

def orthonormal(factor):
    gram_matrix = jnp.dot(factor.T.astype(jnp.float32), factor.astype(jnp.float32), precision=HIGHEST, preferred_element_type=jnp.float32)
    cholesky_lower = jnp.linalg.cholesky(gram_matrix)
    return jax.scipy.linalg.solve_triangular(cholesky_lower, factor.T, lower=True).T

def reference(grad_out, activations, error_feedback, momentum, right_factor):
    outs_grad = grad_out.astype(jnp.float32).reshape(N_DP, TOK_DEV, OUTPUTS)
    inputs_act = activations.astype(jnp.float32).reshape(N_DP, TOK_DEV, INPUTS)
    merged = jnp.einsum('rto,rti->roi', outs_grad, inputs_act, precision=HIGHEST) + error_feedback
    mean_grad = jnp.mean(merged, axis=0)
    right_full = right_factor
    left_factor = None
    for pass_index in range(PASSES):
        left_factor = jnp.dot(mean_grad.astype(jnp.float32), right_full.astype(jnp.float32), precision=HIGHEST, preferred_element_type=jnp.float32)
        left_factor = orthonormal(left_factor)
        right_full = jnp.dot(mean_grad.T.astype(jnp.float32), left_factor.astype(jnp.float32), precision=HIGHEST, preferred_element_type=jnp.float32)
    approx = jnp.dot(left_factor.astype(jnp.float32), right_full.T.astype(jnp.float32), precision=HIGHEST, preferred_element_type=jnp.float32)
    new_error = merged - approx[None]
    new_momentum = (MOMENTUM_RATE * momentum.astype(jnp.float32) + approx).astype(jnp.bfloat16)
    return (new_error, new_momentum, right_full)
```

```python
import jax
import jax.numpy as jnp
from jax import lax
from jax.sharding import PartitionSpec as P

PASSES = 2
MOMENTUM_RATE = 0.9
HIGHEST = lax.Precision.HIGHEST
F32 = jnp.float32


def ring_masks(size):
    masks, mask = [], 1
    while mask < size:
        masks.append(mask)
        mask = 2 * mask + 1
    return masks


def swap(value, axis, mask):
    size = lax.axis_size(axis)
    return lax.ppermute(value, axis, [(i, i ^ mask) for i in range(size)])


def parts_of(array, count, dim=0):
    return jnp.split(array, count, axis=dim) if count > 1 else [array]


def rotations(masks):
    count = 1 << (len(masks).bit_length() - 1)
    return [masks[i:] + masks[:i] for i in range(count)]


def all_reduce(array, axis, masks):
    if not masks:
        return array
    orders = rotations(masks)
    parts = parts_of(array, len(orders))
    for step in range(len(masks)):
        came = [swap(part, axis, order[step]) for part, order in zip(parts, orders)]
        parts = [part + other for part, other in zip(parts, came)]
    return jnp.concatenate(parts, axis=0) if len(parts) > 1 else parts[0]


def all_gather(array, axis, masks):
    if not masks:
        return {0: array}
    orders = rotations(masks)
    held = [{0: part} for part in parts_of(array, len(orders))]
    for step in range(len(masks)):
        fresh = []
        for blocks, order in zip(held, orders):
            keys = sorted(blocks)
            came = swap(jnp.stack([blocks[k] for k in keys]), axis, order[step])
            fresh.append({k ^ order[step]: came[n] for n, k in enumerate(keys)})
        for blocks, extra in zip(held, fresh):
            blocks.update(extra)
    return {k: jnp.concatenate([blocks[k] for blocks in held], axis=0) for k in held[0]}


def span_of(masks):
    keys = [0]
    for mask in masks:
        keys = keys + [k ^ mask for k in keys]
    return sorted(keys)


def to_half(array):
    top = jnp.max(jnp.abs(array))
    power = jnp.where(top > 0, 13.0 - jnp.floor(jnp.log2(jnp.maximum(top, 1e-37))), 0.0)
    power = jnp.clip(power, -100.0, 100.0)
    body = (array * jnp.exp2(power)).astype(jnp.float16)
    tail = jnp.full((16, array.shape[-1]), power, jnp.float16)
    return jnp.concatenate([body, tail], axis=0)


def from_half(message):
    power = message[-1, 0].astype(F32)
    return message[:-16].astype(F32) * jnp.exp2(-power)


def reduce_scatter_half(pieces, axis, masks):
    orders = rotations(masks)
    done = []
    split = {k: parts_of(piece, len(orders)) for k, piece in pieces.items()}
    held = [{k: split[k][n] for k in split} for n in range(len(orders))]
    coords = []
    for order in orders:
        table = {0: ()}
        for mask in order:
            table = {**{k: v + (0,) for k, v in table.items()}, **{k ^ mask: v + (1,) for k, v in table.items()}}
        coords.append(table)
    for step in range(len(masks)):
        arrivals = []
        for blocks, order, table in zip(held, orders, coords):
            away = sorted(k for k in blocks if table[k][step])
            message = jnp.concatenate([blocks[k] for k in away], axis=0)
            arrivals.append((away, swap(to_half(message), axis, order[step])))
        fresh = []
        for blocks, order, (away, message) in zip(held, orders, arrivals):
            came = parts_of(from_half(message), len(away))
            fresh.append({k ^ order[step]: blocks[k ^ order[step]] + came[n] for n, k in enumerate(away)})
        held = fresh
    return jnp.concatenate([blocks[0] for blocks in held], axis=0)


def from_relative(blocks, index, count):
    table = jnp.stack([blocks[k] for k in range(count)])
    order = jnp.bitwise_xor(jnp.arange(count), index)
    return jnp.take(table, order, axis=0)


def dot(a, b, dims, precision=HIGHEST):
    return lax.dot_general(a, b, (dims, ((), ())), precision=precision, preferred_element_type=F32)


def per_device(dp_masks, chip_masks, grad_out, activations, error_feedback, momentum, right_factor):
    replicas, row_blocks = lax.axis_size("dp"), lax.axis_size("rows")
    me_dp, me_row = lax.axis_index("dp"), lax.axis_index("rows")
    error = error_feedback[0]
    inputs = error.shape[1]
    width = inputs // replicas

    tokens = activations.shape[0]
    row_masks = chip_masks + [1]
    gathered = all_gather(activations, "rows", chip_masks)
    gathered.update({k ^ 1: swap(block, "rows", 1) for k, block in list(gathered.items())})
    full_act = from_relative(gathered, me_row, row_blocks)
    full_act = jnp.moveaxis(full_act, 0, 1).reshape(tokens, inputs)
    right_all = all_gather(right_factor, "rows", chip_masks)
    right_all.update({k ^ 1: swap(block, "rows", 1) for k, block in list(right_all.items())})
    right_all = from_relative(right_all, me_row, row_blocks).reshape(inputs, -1)
    right = lax.dynamic_slice_in_dim(right_all, me_dp * width, width, 0)

    merged = lax.dot_general(grad_out, full_act, (((0,), (0,)), ((), ())), preferred_element_type=F32) + error
    pieces = {
        k: lax.dynamic_slice_in_dim(merged, jnp.bitwise_xor(me_dp, k) * width, width, 1)
        for k in span_of(dp_masks)
    }
    mean = reduce_scatter_half(pieces, "dp", dp_masks) / replicas

    own_half = me_row % 2
    for _ in range(PASSES):
        left = all_reduce(dot(mean, right, ((1,), (0,))), "dp", dp_masks)
        term = dot(mean, left, ((0,), (0,)))
        gram = dot(left, left, ((0,), (0,)))
        both = jnp.concatenate([term, gram], axis=0)
        half = both.shape[0] // 2
        keep = lax.dynamic_slice_in_dim(both, own_half * half, half, 0)
        give = lax.dynamic_slice_in_dim(both, (1 - own_half) * half, half, 0)
        keep = all_reduce(keep + swap(give, "rows", 1), "rows", chip_masks)
        other = swap(keep, "rows", 1)
        both = jnp.where(own_half == 0, jnp.concatenate([keep, other]), jnp.concatenate([other, keep]))
        term, gram = both[:width], both[width:]
        lower = jnp.linalg.cholesky(gram)
        right = jax.scipy.linalg.solve_triangular(lower, term.T, lower=True).T
    left = jax.scipy.linalg.solve_triangular(lower, left.T, lower=True).T
    full_right = from_relative(all_gather(right, "dp", dp_masks), me_dp, replicas).reshape(inputs, -1)
    own_rows = lax.dynamic_slice_in_dim(full_right, me_row * right_factor.shape[0], right_factor.shape[0], 0)
    approx = dot(left, full_right, ((1,), (1,)))
    new_error = (merged - approx)[None]
    new_momentum = (MOMENTUM_RATE * momentum.astype(F32) + approx).astype(jnp.bfloat16)
    return (new_error, new_momentum, own_rows)


def solution(mesh):
    replicas, row_blocks = mesh.shape["dp"], mesh.shape["rows"]
    side = 1 << ((replicas.bit_length() - 1) // 2)
    dp_masks = ring_masks(side) + [m * side for m in ring_masks(replicas // side)]
    chip_masks = [2 * m for m in ring_masks(row_blocks // 2)]

    def body(*args):
        return per_device(dp_masks, chip_masks, *args)

    return jax.shard_map(
        body,
        mesh=mesh,
        in_specs=(
            P("dp", "rows"),
            P("dp", "rows"),
            P("dp", "rows", None),
            P("rows", None),
            P("rows", None),
        ),
        out_specs=(P("dp", "rows", None), P("rows", None), P("rows", None)),
        check_vma=False,
    )
```

```python
import jax
import jax.numpy as jnp
from jax import lax
from jax.experimental import pallas as pl
from jax.experimental.pallas import tpu as pltpu
from jax.sharding import PartitionSpec as P

PASSES = 2
MOMENTUM_RATE = 0.9
HIGHEST = lax.Precision.HIGHEST
F32 = jnp.float32


def ring_masks(size):
    masks, mask = [], 1
    while mask < size:
        masks.append(mask)
        mask = 2 * mask + 1
    return masks


def swap(value, axis, mask):
    size = lax.axis_size(axis)
    return lax.ppermute(value, axis, [(i, i ^ mask) for i in range(size)])


def parts_of(array, count, dim=0):
    return jnp.split(array, count, axis=dim) if count > 1 else [array]


def rotations(masks):
    count = 1 << (len(masks).bit_length() - 1)
    return [masks[i:] + masks[:i] for i in range(count)]


def all_reduce(array, axis, masks):
    if not masks:
        return array
    orders = rotations(masks)
    parts = parts_of(array, len(orders))
    for step in range(len(masks)):
        came = [swap(part, axis, order[step]) for part, order in zip(parts, orders)]
        parts = [part + other for part, other in zip(parts, came)]
    return jnp.concatenate(parts, axis=0) if len(parts) > 1 else parts[0]


def all_gather(array, axis, masks):
    if not masks:
        return {0: array}
    orders = rotations(masks)
    held = [{0: part} for part in parts_of(array, len(orders))]
    for step in range(len(masks)):
        fresh = []
        for blocks, order in zip(held, orders):
            keys = sorted(blocks)
            came = swap(jnp.stack([blocks[k] for k in keys]), axis, order[step])
            fresh.append({k ^ order[step]: came[n] for n, k in enumerate(keys)})
        for blocks, extra in zip(held, fresh):
            blocks.update(extra)
    return {k: jnp.concatenate([blocks[k] for blocks in held], axis=0) for k in held[0]}


def span_of(masks):
    keys = [0]
    for mask in masks:
        keys = keys + [k ^ mask for k in keys]
    return sorted(keys)


def to_half(array):
    top = jnp.max(jnp.abs(array))
    power = jnp.where(top > 0, 13.0 - jnp.floor(jnp.log2(jnp.maximum(top, 1e-37))), 0.0)
    power = jnp.clip(power, -100.0, 100.0)
    body = (array * jnp.exp2(power)).astype(jnp.float16)
    tail = jnp.full((16, array.shape[-1]), power, jnp.float16)
    return jnp.concatenate([body, tail], axis=0)


def from_half(message):
    power = message[-1, 0].astype(F32)
    return message[:-16].astype(F32) * jnp.exp2(-power)


def reduce_scatter_half(pieces, axis, masks):
    orders = rotations(masks)
    done = []
    split = {k: parts_of(piece, len(orders)) for k, piece in pieces.items()}
    held = [{k: split[k][n] for k in split} for n in range(len(orders))]
    coords = []
    for order in orders:
        table = {0: ()}
        for mask in order:
            table = {**{k: v + (0,) for k, v in table.items()}, **{k ^ mask: v + (1,) for k, v in table.items()}}
        coords.append(table)
    for step in range(len(masks)):
        arrivals = []
        for blocks, order, table in zip(held, orders, coords):
            away = sorted(k for k in blocks if table[k][step])
            message = jnp.concatenate([blocks[k] for k in away], axis=0)
            arrivals.append((away, swap(to_half(message), axis, order[step])))
        fresh = []
        for blocks, order, (away, message) in zip(held, orders, arrivals):
            came = parts_of(from_half(message), len(away))
            fresh.append({k ^ order[step]: blocks[k ^ order[step]] + came[n] for n, k in enumerate(away)})
        held = fresh
    return jnp.concatenate([blocks[0] for blocks in held], axis=0)


def from_relative(blocks, index, count):
    table = jnp.stack([blocks[k] for k in range(count)])
    order = jnp.bitwise_xor(jnp.arange(count), index)
    return jnp.take(table, order, axis=0)


def dot(a, b, dims, precision=HIGHEST):
    return lax.dot_general(a, b, (dims, ((), ())), precision=precision, preferred_element_type=F32)


def per_device(dp_masks, chip_masks, grad_out, activations, error_feedback, momentum, right_factor):
    replicas, row_blocks = lax.axis_size("dp"), lax.axis_size("rows")
    me_dp, me_row = lax.axis_index("dp"), lax.axis_index("rows")
    error = error_feedback[0]
    inputs = error.shape[1]
    width = inputs // replicas

    tokens = activations.shape[0]
    row_masks = chip_masks + [1]
    gathered = all_gather(activations, "rows", chip_masks)
    gathered.update({k ^ 1: swap(block, "rows", 1) for k, block in list(gathered.items())})
    full_act = from_relative(gathered, me_row, row_blocks)
    full_act = jnp.moveaxis(full_act, 0, 1).reshape(tokens, inputs)
    right_all = all_gather(right_factor, "rows", chip_masks)
    right_all.update({k ^ 1: swap(block, "rows", 1) for k, block in list(right_all.items())})
    right_all = from_relative(right_all, me_row, row_blocks).reshape(inputs, -1)
    right = lax.dynamic_slice_in_dim(right_all, me_dp * width, width, 0)

    merged = lax.dot_general(grad_out, full_act, (((0,), (0,)), ((), ())), preferred_element_type=F32) + error
    pieces = {
        k: lax.dynamic_slice_in_dim(merged, jnp.bitwise_xor(me_dp, k) * width, width, 1)
        for k in span_of(dp_masks)
    }
    mean = reduce_scatter_half(pieces, "dp", dp_masks) / replicas

    own_half = me_row % 2
    for _ in range(PASSES):
        left = all_reduce(dot(mean, right, ((1,), (0,))), "dp", dp_masks)
        term = dot(mean, left, ((0,), (0,)))
        gram = dot(left, left, ((0,), (0,)))
        both = jnp.concatenate([term, gram], axis=0)
        half = both.shape[0] // 2
        keep = lax.dynamic_slice_in_dim(both, own_half * half, half, 0)
        give = lax.dynamic_slice_in_dim(both, (1 - own_half) * half, half, 0)
        keep = all_reduce(keep + swap(give, "rows", 1), "rows", chip_masks)
        other = swap(keep, "rows", 1)
        both = jnp.where(own_half == 0, jnp.concatenate([keep, other]), jnp.concatenate([other, keep]))
        term, gram = both[:width], both[width:]
        lower = jnp.linalg.cholesky(gram)
        right = jax.scipy.linalg.solve_triangular(lower, term.T, lower=True).T
    left = jax.scipy.linalg.solve_triangular(lower, left.T, lower=True).T
    full_right = from_relative(all_gather(right, "dp", dp_masks), me_dp, replicas).reshape(inputs, -1)
    own_rows = lax.dynamic_slice_in_dim(full_right, me_row * right_factor.shape[0], right_factor.shape[0], 0)
    approx = dot(left, full_right, ((1,), (1,)))
    new_error = (merged - approx)[None]
    new_momentum = (MOMENTUM_RATE * momentum.astype(F32) + approx).astype(jnp.bfloat16)
    return (new_error, new_momentum, own_rows)


LEVELS = 32000.0
TAIL = 16
BF16 = jnp.bfloat16


def encode(x):
    top = jnp.max(jnp.abs(x), axis=0, keepdims=True)
    scale = (jnp.maximum(top, 1e-30) * 1.01).astype(BF16)
    ratio = jnp.abs(x) * (1.0 / scale.astype(F32))
    level = jnp.floor(jnp.sqrt(ratio) * LEVELS + 0.5)
    whole = jnp.floor(level * (1.0 / 128.0))
    code = jnp.exp2(whole - 125.0) * (1.0 + (level - whole * 128.0) * (1.0 / 128.0))
    return jnp.where(x < 0, -code, code).astype(BF16), scale


def decode(code, scale):
    code = code.astype(F32)
    size = jnp.abs(code)
    whole = jnp.floor(jnp.log2(size))
    level = (whole + 125.0) * 128.0 + (size * jnp.exp2(-whole) - 1.0) * 128.0
    value = level * level * (scale.astype(F32) * (1.0 / (LEVELS * LEVELS)))
    return jnp.where(code < 0, -value, value)


def put(message, slot, count, x):
    rows = x.shape[0]
    code, scale = encode(x)
    message[slot * rows:(slot + 1) * rows, :] = code
    message[count * rows + slot:count * rows + slot + 1, :] = scale


def take(message, slot, count, rows):
    return decode(message[slot * rows:(slot + 1) * rows, :], message[count * rows + slot:count * rows + slot + 1, :])


def halves(x):
    high = x.astype(BF16)
    return high, (x - high.astype(F32)).astype(BF16)


def mm(a, b, ca, cb, precision=None):
    return lax.dot_general(a, b, (((ca,), (cb,)), ((), ())), precision=precision, preferred_element_type=F32)


def stage_kernel(ids, g_ref, a_ref, b_ref, e_ref, merged_ref, mx_ref, my_ref):
    k = pl.program_id(0)
    q = jnp.bitwise_xor(ids[0], k)
    a = jnp.where(q // 2 == ids[2], a_ref[...], b_ref[...])
    value = mm(g_ref[...], a, 0, 0) + e_ref[0]
    merged_ref[...] = value
    half = value.shape[0] // 2

    @pl.when(k == 1)
    def _():
        put(mx_ref, 0, 2, value[:half])

    @pl.when(k == 2)
    def _():
        put(my_ref, 0, 2, value[half:])

    @pl.when(k == 3)
    def _():
        put(mx_ref, 1, 2, value[:half])
        put(my_ref, 1, 2, value[half:])


def stage(ids, grad, a, b, error, which, sub):
    rows, tokens = grad.shape[1], grad.shape[0]
    per_chunk = 4

    def error_at(k, ids):
        return (0, 0, jnp.bitwise_xor(ids[1], which) * per_chunk + jnp.bitwise_xor(ids[0], k))

    grid_spec = pltpu.PrefetchScalarGridSpec(
        num_scalar_prefetch=1,
        grid=(per_chunk,),
        in_specs=[
            pl.BlockSpec((tokens, rows), lambda k, ids: (0, 0)),
            pl.BlockSpec((tokens, sub), lambda k, ids: (0, jnp.bitwise_xor(ids[0], k) % 2)),
            pl.BlockSpec((tokens, sub), lambda k, ids: (0, jnp.bitwise_xor(ids[0], k) % 2)),
            pl.BlockSpec((1, rows, sub), error_at),
        ],
        out_specs=[
            pl.BlockSpec((rows, sub), lambda k, ids: (0, jnp.bitwise_xor(ids[0], k))),
            pl.BlockSpec((rows + TAIL, sub), lambda k, ids: (0, 0)),
            pl.BlockSpec((rows + TAIL, sub), lambda k, ids: (0, 0)),
        ],
    )
    message = jax.ShapeDtypeStruct((rows + TAIL, sub), BF16)
    return pl.pallas_call(
        stage_kernel,
        grid_spec=grid_spec,
        out_shape=[jax.ShapeDtypeStruct((rows, per_chunk * sub), F32), message, message],
        cost_estimate=pl.CostEstimate(flops=2 * rows * tokens * 4 * sub, bytes_accessed=rows * sub * 40, transcendentals=0),
        name="stage",
    )(ids, grad, a, b, error)


def second_kernel(ids, rx_ref, ry_ref, top_ref, low_ref, my_ref, mx_ref):
    half = top_ref.shape[0]
    put(my_ref, 0, 1, top_ref[...] + take(rx_ref, 1, 2, half))
    put(mx_ref, 0, 1, low_ref[...] + take(ry_ref, 1, 2, half))


def second(ids, rx, ry, merged, sub):
    half = merged.shape[0] // 2
    grid_spec = pltpu.PrefetchScalarGridSpec(
        num_scalar_prefetch=1,
        grid=(1,),
        in_specs=[
            pl.BlockSpec(rx.shape, lambda k, ids: (0, 0)),
            pl.BlockSpec(ry.shape, lambda k, ids: (0, 0)),
            pl.BlockSpec((half, sub), lambda k, ids: (0, jnp.bitwise_xor(ids[0], 2))),
            pl.BlockSpec((half, sub), lambda k, ids: (1, jnp.bitwise_xor(ids[0], 1))),
        ],
        out_specs=[pl.BlockSpec((half + TAIL, sub), lambda k, ids: (0, 0))] * 2,
    )
    return pl.pallas_call(
        second_kernel,
        grid_spec=grid_spec,
        out_shape=[jax.ShapeDtypeStruct((half + TAIL, sub), BF16)] * 2,
        cost_estimate=pl.CostEstimate(flops=half * sub * 80, bytes_accessed=half * sub * 20, transcendentals=0),
        name="second",
    )(ids, rx, ry, merged, merged)


def third_kernel(scale, ids, rx_ref, ry_ref, sy_ref, sx_ref, own_ref, high_ref, low_ref):
    half = own_ref.shape[0] // 2
    top = own_ref[:half] + take(rx_ref, 0, 2, half) + take(sy_ref, 0, 1, half)
    low = own_ref[half:] + take(ry_ref, 0, 2, half) + take(sx_ref, 0, 1, half)
    high_ref[:half], low_ref[:half] = halves(top * scale)
    high_ref[half:], low_ref[half:] = halves(low * scale)


def third(ids, rx, ry, sy, sx, merged, sub, scale):
    rows = merged.shape[0]
    whole = lambda k, ids: (0, 0)
    grid_spec = pltpu.PrefetchScalarGridSpec(
        num_scalar_prefetch=1,
        grid=(1,),
        in_specs=[
            pl.BlockSpec(rx.shape, whole),
            pl.BlockSpec(ry.shape, whole),
            pl.BlockSpec(sy.shape, whole),
            pl.BlockSpec(sx.shape, whole),
            pl.BlockSpec((rows, sub), lambda k, ids: (0, ids[0])),
        ],
        out_specs=[pl.BlockSpec((rows, sub), whole)] * 2,
    )
    return pl.pallas_call(
        lambda *refs: third_kernel(scale, *refs),
        grid_spec=grid_spec,
        out_shape=[jax.ShapeDtypeStruct((rows, sub), BF16)] * 2,
        cost_estimate=pl.CostEstimate(flops=rows * sub * 80, bytes_accessed=rows * sub * 20, transcendentals=0),
        name="third",
    )(ids, rx, ry, sy, sx, merged)


def plain_call(kernel, out_shape, ids, args, name, flops, scratch=()):
    return pl.pallas_call(
        kernel,
        in_specs=[pl.BlockSpec(memory_space=pltpu.SMEM)] + [pl.BlockSpec(memory_space=pltpu.VMEM)] * len(args),
        out_specs=[pl.BlockSpec(memory_space=pltpu.VMEM)] * len(out_shape),
        out_shape=out_shape,
        scratch_shapes=list(scratch),
        cost_estimate=pl.CostEstimate(flops=flops, bytes_accessed=flops // 128, transcendentals=0),
        name=name,
    )(ids, *args)


def times(high, low, right_high, right_low, axis):
    rank = right_high.shape[1 - axis]
    both = mm(high, jnp.concatenate([right_high, right_low], axis=1 - axis), 1, axis)
    return both[:, :rank] + both[:, rank:] + mm(low, right_high, 1, axis)


def first_left_kernel(ids, *refs):
    means, rights, (top, low) = refs[:8], refs[8:12], refs[12:]
    total = None
    for s in range(4):
        right_high, right_low = halves(rights[s][...])
        term = times(means[2 * s][...], means[2 * s + 1][...], right_high, right_low, 0)
        total = term if total is None else total + term
    half = total.shape[0] // 2
    top[...] = total[:half]
    low[...] = total[half:]


def next_left_kernel(ids, *refs):
    means, (own0, own1, other0, other1), (top, low), (right,) = refs[:8], refs[8:12], refs[12:14], refs[14:]
    width = right.shape[2]
    rows = own0.shape[0]
    z, c = ids[1], ids[2]
    right[c, :rows] = own0[:, :width]
    right[c, rows:] = own1[:, :width]
    right[1 - c, :rows] = other0[:, :width]
    right[1 - c, rows:] = other1[:, :width]
    sub = width // 2
    total = None
    for s in range(4):
        chunk = jnp.bitwise_xor(z, s)
        part = right[chunk // 2, :, pl.ds(pl.multiple_of((chunk % 2) * sub, sub), sub)]
        right_high, right_low = halves(part)
        term = times(means[2 * s][...], means[2 * s + 1][...], right_high, right_low, 1)
        total = term if total is None else total + term
    half = total.shape[0] // 2
    top[...] = total[:half]
    low[...] = total[half:]


def right_kernel(solved, ids, *refs):
    means, (a0, b0, a1, b1), rest = refs[:8], refs[8:12], refs[12:]
    inverse = rest[0] if solved else None
    left_ref, keep, give, both = rest[1:] if solved else rest
    left = jnp.concatenate([a0[...] + b0[...], a1[...] + b1[...]], axis=0)
    if solved:
        left = mm(left, inverse[...], 1, 1, HIGHEST)
    left_ref[...] = left
    rank = left.shape[1]
    gram = mm(left, left, 0, 0, HIGHEST)
    left_high, left_low = halves(left)
    pair = jnp.concatenate([left_high, left_low], axis=1)
    z, c = ids[1], ids[2]
    sub = means[0].shape[1]
    for s in range(4):
        chunk = jnp.bitwise_xor(z, s)
        two = mm(pair, means[2 * s][...], 0, 0)
        term = two[:rank] + two[rank:] + mm(left_high, means[2 * s + 1][...], 0, 0)
        both[chunk // 2, :, pl.ds(pl.multiple_of((chunk % 2) * sub, sub), sub)] = term
    keep[:, :2 * sub] = both[c]
    keep[:, 2 * sub:] = gram
    give[:, :2 * sub] = both[1 - c]
    give[:, 2 * sub:] = gram


def final_kernel(ids, inverse, left, own0, own1, other0, other1, m0, m1, m2, m3, momentum, *rest):
    error_out, momentum_out, base, right = rest[-4:]
    s = pl.program_id(0)
    z, c = ids[1], ids[2]
    rows, width = own0.shape
    sub = width // 2

    @pl.when(s == 0)
    def _():
        solved = mm(left[...], inverse[...], 1, 1, HIGHEST)
        base[...] = mm(solved, inverse[...], 1, 0, HIGHEST)
        right[c, :rows] = own0[...]
        right[c, rows:] = own1[...]
        right[1 - c, :rows] = other0[...]
        right[1 - c, rows:] = other1[...]

    chunk = jnp.bitwise_xor(z, s)
    part = right[chunk // 2, :, pl.ds(pl.multiple_of((chunk % 2) * sub, sub), sub)]
    base_high, base_low = halves(base[...])
    part_high, part_low = halves(part)
    approx = mm(base_high, part_high, 1, 0) + mm(base_high, part_low, 1, 0) + mm(base_low, part_high, 1, 0)
    for t, merged in enumerate((m0, m1, m2, m3)):
        @pl.when(s == t)
        def _(merged=merged):
            error_out[0] = merged[...] - approx

    momentum_out[...] = (MOMENTUM_RATE * momentum[...].astype(F32) + approx).astype(BF16)


def final(ids, inverse, left, rights, merged, momentum, carried, which):
    rows, inputs = momentum.shape
    sub = merged[0].shape[1] // 4
    column = lambda s, ids: (0, jnp.bitwise_xor(ids[1], s) * 4 + jnp.bitwise_xor(ids[0], which))
    column3 = lambda s, ids: (0,) + column(s, ids)
    still = lambda s, ids: (0, 0)
    mine = lambda s, ids: (0, jnp.bitwise_xor(ids[0], which))
    whole = [inverse, left] + list(rights)
    grid_spec = pltpu.PrefetchScalarGridSpec(
        num_scalar_prefetch=1,
        grid=(4,),
        in_specs=[pl.BlockSpec(x.shape, still) for x in whole]
        + [pl.BlockSpec((rows, sub), mine)] * 4
        + [pl.BlockSpec((rows, sub), column)]
        + [pl.BlockSpec(memory_space=pl.ANY)] * len(carried),
        out_specs=[pl.BlockSpec((1, rows, sub), column3), pl.BlockSpec((rows, sub), column)],
        scratch_shapes=[pltpu.VMEM(left.shape, F32), pltpu.VMEM((2, 2 * rights[0].shape[0], rights[0].shape[1]), F32)],
    )
    first = 1 + len(whole) + 5
    return pl.pallas_call(
        final_kernel,
        grid_spec=grid_spec,
        out_shape=[jax.ShapeDtypeStruct((1, rows, inputs), F32), jax.ShapeDtypeStruct((rows, inputs), BF16)],
        input_output_aliases={first + n: n for n in range(len(carried))},
        cost_estimate=pl.CostEstimate(flops=2 * rows * rows * sub * 4, bytes_accessed=rows * sub * 48, transcendentals=0),
        name="final",
    )(ids, *whole, *merged, momentum, *carried)


def own_right_kernel(ids, inverse, *refs):
    blocks, out = refs[:-1], refs[-1]
    r, z, c = ids[0], ids[1], ids[2]
    rows, width = blocks[0].shape
    sub = width // 2
    offset = pl.multiple_of((z % 2) * sub, sub)
    for n in range(2):
        need = jnp.bitwise_xor(2 * c + n, r)
        for k in range(4):
            for side in range(2):
                @pl.when((need == k) & ((z // 2 == c) == (side == 0)))
                def _(k=k, side=side, n=n):
                    top = blocks[4 * k + 2 * side][:, pl.ds(offset, sub)]
                    low = blocks[4 * k + 2 * side + 1][:, pl.ds(offset, sub)]
                    piece = jnp.concatenate([top, low], axis=0)
                    out[n * sub:(n + 1) * sub, :] = mm(piece, inverse[...], 0, 1, HIGHEST)


def per_device_square(x_mask, y_mask, a_mask, b_mask, grad_out, activations, error_feedback, momentum, right_factor):
    replicas = lax.axis_size("dp")
    me_dp, me_row = lax.axis_index("dp"), lax.axis_index("rows")
    ids = jnp.stack([me_dp, me_row // 2, me_row % 2]).astype(jnp.int32)
    rank = right_factor.shape[1]
    rows = grad_out.shape[1]
    block = activations.shape[1]
    sub = 2 * block // replicas
    over_x = lambda v: swap(v, "dp", x_mask)
    over_y = lambda v: swap(v, "dp", y_mask)
    over_a = lambda v: swap(v, "rows", a_mask)
    over_b = lambda v: swap(v, "rows", b_mask)
    over_c = lambda v: swap(v, "rows", 1)

    half_tokens = activations.shape[0] // 2
    act = {0: activations, 1: over_a(activations), 3: over_b(activations)}
    act[2] = jnp.concatenate([over_b(act[1][:half_tokens]), over_a(act[3][half_tokens:])], axis=0)

    other = over_c(right_factor)
    mine = jnp.where(me_dp // 2 == me_row % 2, right_factor, other)
    mine = lax.dynamic_slice_in_dim(mine, (me_dp % 2) * sub, sub, 0)
    rights = {0: mine, 1: over_a(mine), 3: over_b(mine)}
    rights[2] = over_b(rights[1])

    merged, means = {}, {}
    for s in (0, 1, 3, 2):
        merged[s], mx, my = stage(ids, grad_out, act[s], over_c(act[s]), error_feedback, s, sub)
        rx, ry = over_x(mx), over_y(my)
        ny, nx = second(ids, rx, ry, merged[s], sub)
        means[s] = third(ids, rx, ry, over_y(ny), over_x(nx), merged[s], sub, 1.0 / replicas)
    flat = [part for s in range(4) for part in means[s]]
    shape = lambda *dims: jax.ShapeDtypeStruct(dims, F32)
    left_flops = 6 * rows * 4 * sub * rank

    inverse = None
    for pass_index in range(PASSES):
        outs = [shape(rows // 2, rank)] * 2
        if pass_index == 0:
            p0, p1 = plain_call(first_left_kernel, outs, ids, flat + [rights[s] for s in range(4)], "left", left_flops)
        else:
            p0, p1 = plain_call(
                next_left_kernel, outs, ids, flat + [f0, f1, over_c(f0), over_c(f1)], "left", left_flops,
                [pltpu.VMEM((2, rank, 2 * sub), F32)],
            )
        p0, p1 = p0 + over_x(p0), p1 + over_y(p1)
        operands = flat + [p0, over_y(p0), p1, over_x(p1)]
        if pass_index:
            operands.append(inverse)
        left, keep, give = plain_call(
            lambda *refs, solved=pass_index > 0: right_kernel(solved, *refs),
            [shape(rows, rank), shape(rank, 2 * sub + rank), shape(rank, 2 * sub + rank)],
            ids, operands, "right", left_flops, [pltpu.VMEM((2, rank, 2 * sub), F32)],
        )
        total = keep + over_c(give)
        f0, f1 = total[:rank // 2], total[rank // 2:]
        f0, f1 = f0 + over_a(f0), f1 + over_b(f1)
        f0, f1 = f0 + over_b(f0), f1 + over_a(f1)
        gram = jnp.concatenate([f0[:, 2 * sub:], f1[:, 2 * sub:]], axis=0)
        lower = jnp.linalg.cholesky(gram)
        inverse = jax.scipy.linalg.solve_triangular(lower, jnp.eye(rank, dtype=F32), lower=True)

    g0, g1 = f0[:, :2 * sub], f1[:, :2 * sub]
    x0, y1 = over_x(g0), over_y(g1)
    pieces = {0: (g0, g1), 1: (x0, over_x(g1)), 2: (over_y(g0), y1), 3: (over_y(x0), over_x(y1))}
    carried, every = [], []
    for k in range(4):
        own0, own1 = pieces[k]
        blocks = [own0, own1, over_c(own0), over_c(own1)]
        every += blocks
        carried = final(ids, inverse, left, blocks, [merged[s] for s in range(4)], momentum, carried, k)
    own_rows = plain_call(
        own_right_kernel, [shape(rows, rank)], ids, [inverse] + every, "own_right", 2 * rows * rank * rank * 6
    )[0]
    return carried[0], carried[1], own_rows


def solution(mesh):
    replicas, row_blocks = mesh.shape["dp"], mesh.shape["rows"]
    side = 1 << ((replicas.bit_length() - 1) // 2)
    dp_masks = ring_masks(side) + [m * side for m in ring_masks(replicas // side)]
    chip_masks = [2 * m for m in ring_masks(row_blocks // 2)]

    square = len(dp_masks) == 2 and len(chip_masks) == 2

    def body(*args):
        sub = 2 * args[1].shape[1] // replicas
        if square and sub % 128 == 0 and args[4].shape[1] % 128 == 0:
            return per_device_square(*dp_masks, *chip_masks, *args)
        return per_device(dp_masks, chip_masks, *args)

    return jax.shard_map(
        body,
        mesh=mesh,
        in_specs=(
            P("dp", "rows"),
            P("dp", "rows"),
            P("dp", "rows", None),
            P("rows", None),
            P("rows", None),
        ),
        out_specs=(P("dp", "rows", None), P("rows", None), P("rows", None)),
        check_vma=False,
    )
```

```python
import math

import jax
import jax.numpy as jnp
from jax import lax
from jax.experimental import pallas as pl
from jax.experimental.pallas import tpu as pltpu
from jax.sharding import PartitionSpec as P

PASSES = 2
MOMENTUM_RATE = 0.9
HIGHEST = lax.Precision.HIGHEST
F32 = jnp.float32


def ring_masks(size):
    masks, mask = [], 1
    while mask < size:
        masks.append(mask)
        mask = 2 * mask + 1
    return masks


def swap(value, axis, mask):
    size = lax.axis_size(axis)
    return lax.ppermute(value, axis, [(i, i ^ mask) for i in range(size)])


def parts_of(array, count, dim=0):
    return jnp.split(array, count, axis=dim) if count > 1 else [array]


def rotations(masks):
    count = 1 << (len(masks).bit_length() - 1)
    return [masks[i:] + masks[:i] for i in range(count)]


def all_reduce(array, axis, masks):
    if not masks:
        return array
    orders = rotations(masks)
    parts = parts_of(array, len(orders))
    for step in range(len(masks)):
        came = [swap(part, axis, order[step]) for part, order in zip(parts, orders)]
        parts = [part + other for part, other in zip(parts, came)]
    return jnp.concatenate(parts, axis=0) if len(parts) > 1 else parts[0]


def all_gather(array, axis, masks):
    if not masks:
        return {0: array}
    orders = rotations(masks)
    held = [{0: part} for part in parts_of(array, len(orders))]
    for step in range(len(masks)):
        fresh = []
        for blocks, order in zip(held, orders):
            keys = sorted(blocks)
            came = swap(jnp.stack([blocks[k] for k in keys]), axis, order[step])
            fresh.append({k ^ order[step]: came[n] for n, k in enumerate(keys)})
        for blocks, extra in zip(held, fresh):
            blocks.update(extra)
    return {k: jnp.concatenate([blocks[k] for blocks in held], axis=0) for k in held[0]}


def span_of(masks):
    keys = [0]
    for mask in masks:
        keys = keys + [k ^ mask for k in keys]
    return sorted(keys)


def to_half(array):
    top = jnp.max(jnp.abs(array))
    power = jnp.where(top > 0, 13.0 - jnp.floor(jnp.log2(jnp.maximum(top, 1e-37))), 0.0)
    power = jnp.clip(power, -100.0, 100.0)
    body = (array * jnp.exp2(power)).astype(jnp.float16)
    tail = jnp.full((16, array.shape[-1]), power, jnp.float16)
    return jnp.concatenate([body, tail], axis=0)


def from_half(message):
    power = message[-1, 0].astype(F32)
    return message[:-16].astype(F32) * jnp.exp2(-power)


def reduce_scatter_half(pieces, axis, masks):
    orders = rotations(masks)
    done = []
    split = {k: parts_of(piece, len(orders)) for k, piece in pieces.items()}
    held = [{k: split[k][n] for k in split} for n in range(len(orders))]
    coords = []
    for order in orders:
        table = {0: ()}
        for mask in order:
            table = {**{k: v + (0,) for k, v in table.items()}, **{k ^ mask: v + (1,) for k, v in table.items()}}
        coords.append(table)
    for step in range(len(masks)):
        arrivals = []
        for blocks, order, table in zip(held, orders, coords):
            away = sorted(k for k in blocks if table[k][step])
            message = jnp.concatenate([blocks[k] for k in away], axis=0)
            arrivals.append((away, swap(to_half(message), axis, order[step])))
        fresh = []
        for blocks, order, (away, message) in zip(held, orders, arrivals):
            came = parts_of(from_half(message), len(away))
            fresh.append({k ^ order[step]: blocks[k ^ order[step]] + came[n] for n, k in enumerate(away)})
        held = fresh
    return jnp.concatenate([blocks[0] for blocks in held], axis=0)


def from_relative(blocks, index, count):
    table = jnp.stack([blocks[k] for k in range(count)])
    order = jnp.bitwise_xor(jnp.arange(count), index)
    return jnp.take(table, order, axis=0)


def dot(a, b, dims, precision=HIGHEST):
    return lax.dot_general(a, b, (dims, ((), ())), precision=precision, preferred_element_type=F32)


def per_device(dp_masks, chip_masks, grad_out, activations, error_feedback, momentum, right_factor):
    replicas, row_blocks = lax.axis_size("dp"), lax.axis_size("rows")
    me_dp, me_row = lax.axis_index("dp"), lax.axis_index("rows")
    error = error_feedback[0]
    inputs = error.shape[1]
    width = inputs // replicas

    tokens = activations.shape[0]
    row_masks = chip_masks + [1]
    gathered = all_gather(activations, "rows", chip_masks)
    gathered.update({k ^ 1: swap(block, "rows", 1) for k, block in list(gathered.items())})
    full_act = from_relative(gathered, me_row, row_blocks)
    full_act = jnp.moveaxis(full_act, 0, 1).reshape(tokens, inputs)
    right_all = all_gather(right_factor, "rows", chip_masks)
    right_all.update({k ^ 1: swap(block, "rows", 1) for k, block in list(right_all.items())})
    right_all = from_relative(right_all, me_row, row_blocks).reshape(inputs, -1)
    right = lax.dynamic_slice_in_dim(right_all, me_dp * width, width, 0)

    merged = lax.dot_general(grad_out, full_act, (((0,), (0,)), ((), ())), preferred_element_type=F32) + error
    pieces = {
        k: lax.dynamic_slice_in_dim(merged, jnp.bitwise_xor(me_dp, k) * width, width, 1)
        for k in span_of(dp_masks)
    }
    mean = reduce_scatter_half(pieces, "dp", dp_masks) / replicas

    own_half = me_row % 2
    for _ in range(PASSES):
        left = all_reduce(dot(mean, right, ((1,), (0,))), "dp", dp_masks)
        term = dot(mean, left, ((0,), (0,)))
        gram = dot(left, left, ((0,), (0,)))
        both = jnp.concatenate([term, gram], axis=0)
        half = both.shape[0] // 2
        keep = lax.dynamic_slice_in_dim(both, own_half * half, half, 0)
        give = lax.dynamic_slice_in_dim(both, (1 - own_half) * half, half, 0)
        keep = all_reduce(keep + swap(give, "rows", 1), "rows", chip_masks)
        other = swap(keep, "rows", 1)
        both = jnp.where(own_half == 0, jnp.concatenate([keep, other]), jnp.concatenate([other, keep]))
        term, gram = both[:width], both[width:]
        lower = jnp.linalg.cholesky(gram)
        right = jax.scipy.linalg.solve_triangular(lower, term.T, lower=True).T
    left = jax.scipy.linalg.solve_triangular(lower, left.T, lower=True).T
    full_right = from_relative(all_gather(right, "dp", dp_masks), me_dp, replicas).reshape(inputs, -1)
    own_rows = lax.dynamic_slice_in_dim(full_right, me_row * right_factor.shape[0], right_factor.shape[0], 0)
    approx = dot(left, full_right, ((1,), (1,)))
    new_error = (merged - approx)[None]
    new_momentum = (MOMENTUM_RATE * momentum.astype(F32) + approx).astype(jnp.bfloat16)
    return (new_error, new_momentum, own_rows)


LEVELS = 32000.0
TAIL = 16
VMEM_LIMIT = 24 << 20
BF16 = jnp.bfloat16


def encode(x):
    size = jnp.abs(x)
    top = jnp.max(size, axis=0, keepdims=True)
    scale = (jnp.maximum(top, 1e-30) * 1.01).astype(BF16)
    ratio = size * (1.0 / scale.astype(F32))
    root = ratio * lax.rsqrt(ratio + 1e-24)
    code = jnp.exp2(root * (LEVELS / 128.0) - 125.0)
    return jnp.where(x < 0, -code, code).astype(BF16), scale


def decode(code, scale):
    code = code.astype(F32)
    level = jnp.log(jnp.abs(code)) * (128.0 / math.log(2.0)) + 125.0 * 128.0
    value = level * level * (scale.astype(F32) * (1.0 / (LEVELS * LEVELS)))
    return jnp.where(code < 0, -value, value)


def put(message, slot, count, x):
    rows = x.shape[0]
    code, scale = encode(x)
    message[slot * rows:(slot + 1) * rows, :] = code
    message[count * rows + slot:count * rows + slot + 1, :] = scale


def take(message, slot, count, rows):
    return decode(message[slot * rows:(slot + 1) * rows, :], message[count * rows + slot:count * rows + slot + 1, :])


def halves(x):
    high = x.astype(BF16)
    return high, (x - high.astype(F32)).astype(BF16)


def mm(a, b, ca, cb, precision=None):
    return lax.dot_general(a, b, (((ca,), (cb,)), ((), ())), precision=precision, preferred_element_type=F32)


def params():
    return pltpu.CompilerParams(vmem_limit_bytes=VMEM_LIMIT)


def stage_kernel(count, ids, gt_ref, *refs):
    acts, (e_ref, merged_ref, mx_ref, my_ref) = refs[:2 * count], refs[2 * count:]
    step = pl.program_id(0)
    k = step % 4
    q = jnp.bitwise_xor(ids[0], k)
    sub = e_ref.shape[2]
    half = e_ref.shape[1] // 2
    columns = pl.ds(pl.multiple_of((q % 2) * sub, sub), sub)
    mine = q // 2 == ids[2]
    for n in range(count):
        @pl.when(step // 4 == n)
        def _(n=n):
            a = jnp.where(mine, acts[2 * n][:, columns], acts[2 * n + 1][:, columns])
            value = mm(gt_ref[...], a, 1, 0) + e_ref[0]
            merged_ref[...] = value

            @pl.when(k == 1)
            def _():
                put(mx_ref, 2 * n, 2 * count, value[:half])

            @pl.when(k == 2)
            def _():
                put(my_ref, 2 * n, 2 * count, value[half:])

            @pl.when(k == 3)
            def _():
                put(mx_ref, 2 * n + 1, 2 * count, value[:half])
                put(my_ref, 2 * n + 1, 2 * count, value[half:])


def stage(ids, grad_t, acts, error, chunks, sub):
    rows, tokens = grad_t.shape
    count = len(chunks)

    def chunk_of(step):
        return chunks[0] + (step // 4) * (chunks[-1] - chunks[0])

    def error_at(step, ids):
        return (0, 0, jnp.bitwise_xor(ids[1], chunk_of(step)) * 4 + jnp.bitwise_xor(ids[0], step % 4))

    still = lambda step, ids: (0, 0)
    length = count * rows + TAIL
    grid_spec = pltpu.PrefetchScalarGridSpec(
        num_scalar_prefetch=1,
        grid=(4 * count,),
        in_specs=[pl.BlockSpec((rows, tokens), still)]
        + [pl.BlockSpec(a.shape, still) for a in acts]
        + [pl.BlockSpec((1, rows, sub), error_at)],
        out_specs=[
            pl.BlockSpec((rows, sub), lambda step, ids: (0, (step // 4) * 4 + jnp.bitwise_xor(ids[0], step % 4))),
            pl.BlockSpec((length, sub), still),
            pl.BlockSpec((length, sub), still),
        ],
    )
    message = jax.ShapeDtypeStruct((length, sub), BF16)
    return pl.pallas_call(
        lambda *refs: stage_kernel(count, *refs),
        grid_spec=grid_spec,
        out_shape=[jax.ShapeDtypeStruct((rows, count * 4 * sub), F32), message, message],
        cost_estimate=pl.CostEstimate(
            flops=8 * count * rows * tokens * sub, bytes_accessed=count * rows * sub * 40, transcendentals=0
        ),
        compiler_params=params(),
        name="stage",
    )(ids, grad_t, *acts, error)


def second_kernel(count, ids, rx_ref, ry_ref, *refs):
    blocks, (my_ref, mx_ref) = refs[:-2], refs[-2:]
    half = blocks[0].shape[0]
    for n in range(count):
        put(my_ref, n, count, blocks[2 * n][...] + take(rx_ref, 2 * n + 1, 2 * count, half))
        put(mx_ref, n, count, blocks[2 * n + 1][...] + take(ry_ref, 2 * n + 1, 2 * count, half))


def second(ids, rx, ry, merged, sub, count):
    half = merged.shape[0] // 2
    still = lambda k, ids: (0, 0)
    blocks = []
    for n in range(count):
        blocks.append(pl.BlockSpec((half, sub), lambda k, ids, n=n: (0, 4 * n + jnp.bitwise_xor(ids[0], 2))))
        blocks.append(pl.BlockSpec((half, sub), lambda k, ids, n=n: (1, 4 * n + jnp.bitwise_xor(ids[0], 1))))
    length = count * half + TAIL
    grid_spec = pltpu.PrefetchScalarGridSpec(
        num_scalar_prefetch=1,
        grid=(1,),
        in_specs=[pl.BlockSpec(rx.shape, still), pl.BlockSpec(ry.shape, still)] + blocks,
        out_specs=[pl.BlockSpec((length, sub), still)] * 2,
    )
    return pl.pallas_call(
        lambda *refs: second_kernel(count, *refs),
        grid_spec=grid_spec,
        out_shape=[jax.ShapeDtypeStruct((length, sub), BF16)] * 2,
        cost_estimate=pl.CostEstimate(flops=count * half * sub * 80, bytes_accessed=count * half * sub * 20, transcendentals=0),
        compiler_params=params(),
        name="second",
    )(ids, rx, ry, *[merged] * (2 * count))


def third_kernel(scale, count, ids, rx_ref, ry_ref, sy_ref, sx_ref, *refs):
    blocks, outs = refs[:count], refs[count:]
    half = blocks[0].shape[0] // 2
    for n in range(count):
        own, high_ref, low_ref = blocks[n], outs[2 * n], outs[2 * n + 1]
        top = own[:half] + take(rx_ref, 2 * n, 2 * count, half) + take(sy_ref, n, count, half)
        low = own[half:] + take(ry_ref, 2 * n, 2 * count, half) + take(sx_ref, n, count, half)
        high_ref[:half], low_ref[:half] = halves(top * scale)
        high_ref[half:], low_ref[half:] = halves(low * scale)


def third(ids, rx, ry, sy, sx, merged, sub, count, scale):
    rows = merged.shape[0]
    still = lambda k, ids: (0, 0)
    grid_spec = pltpu.PrefetchScalarGridSpec(
        num_scalar_prefetch=1,
        grid=(1,),
        in_specs=[pl.BlockSpec(x.shape, still) for x in (rx, ry, sy, sx)]
        + [pl.BlockSpec((rows, sub), lambda k, ids, n=n: (0, 4 * n + ids[0])) for n in range(count)],
        out_specs=[pl.BlockSpec((rows, sub), still)] * (2 * count),
    )
    return pl.pallas_call(
        lambda *refs: third_kernel(scale, count, *refs),
        grid_spec=grid_spec,
        out_shape=[jax.ShapeDtypeStruct((rows, sub), BF16)] * (2 * count),
        cost_estimate=pl.CostEstimate(flops=count * rows * sub * 80, bytes_accessed=count * rows * sub * 20, transcendentals=0),
        compiler_params=params(),
        name="third",
    )(ids, rx, ry, sy, sx, *[merged] * count)


def plain_call(kernel, out_shape, ids, args, name, flops, scratch=()):
    return pl.pallas_call(
        kernel,
        in_specs=[pl.BlockSpec(memory_space=pltpu.SMEM)] + [pl.BlockSpec(memory_space=pltpu.VMEM)] * len(args),
        out_specs=[pl.BlockSpec(memory_space=pltpu.VMEM)] * len(out_shape),
        out_shape=out_shape,
        scratch_shapes=list(scratch),
        cost_estimate=pl.CostEstimate(flops=flops, bytes_accessed=flops // 128, transcendentals=0),
        compiler_params=params(),
        name=name,
    )(ids, *args)


def times(high, low, right_high, right_low, axis):
    rank = right_high.shape[1 - axis]
    both = mm(high, jnp.concatenate([right_high, right_low], axis=1 - axis), 1, axis)
    return both[:, :rank] + both[:, rank:] + mm(low, right_high, 1, axis)


def first_left_kernel(ids, *refs):
    means, rights, (top, low) = refs[:8], refs[8:12], refs[12:]
    total = None
    for s in range(4):
        right_high, right_low = halves(rights[s][...])
        term = times(means[2 * s][...], means[2 * s + 1][...], right_high, right_low, 0)
        total = term if total is None else total + term
    half = total.shape[0] // 2
    top[...] = total[:half]
    low[...] = total[half:]


def next_left_kernel(ids, *refs):
    means, (own0, own1, other0, other1), (top, low), (right,) = refs[:8], refs[8:12], refs[12:14], refs[14:]
    width = right.shape[2]
    rows = own0.shape[0]
    z, c = ids[1], ids[2]
    right[c, :rows] = own0[:, :width]
    right[c, rows:] = own1[:, :width]
    right[1 - c, :rows] = other0[:, :width]
    right[1 - c, rows:] = other1[:, :width]
    sub = width // 2
    total = None
    for s in range(4):
        chunk = jnp.bitwise_xor(z, s)
        part = right[chunk // 2, :, pl.ds(pl.multiple_of((chunk % 2) * sub, sub), sub)]
        right_high, right_low = halves(part)
        term = times(means[2 * s][...], means[2 * s + 1][...], right_high, right_low, 1)
        total = term if total is None else total + term
    half = total.shape[0] // 2
    top[...] = total[:half]
    low[...] = total[half:]


def right_kernel(solved, ids, *refs):
    means, (a0, b0, a1, b1), rest = refs[:8], refs[8:12], refs[12:]
    inverse = rest[0] if solved else None
    left_ref, keep, give, both = rest[1:] if solved else rest
    left = jnp.concatenate([a0[...] + b0[...], a1[...] + b1[...]], axis=0)
    if solved:
        left = mm(left, inverse[...], 1, 1, HIGHEST)
    left_ref[...] = left
    rank = left.shape[1]
    gram = mm(left, left, 0, 0, HIGHEST)
    left_high, left_low = halves(left)
    pair = jnp.concatenate([left_high, left_low], axis=1)
    z, c = ids[1], ids[2]
    sub = means[0].shape[1]
    for s in range(4):
        chunk = jnp.bitwise_xor(z, s)
        two = mm(pair, means[2 * s][...], 0, 0)
        term = two[:rank] + two[rank:] + mm(left_high, means[2 * s + 1][...], 0, 0)
        both[chunk // 2, :, pl.ds(pl.multiple_of((chunk % 2) * sub, sub), sub)] = term
    keep[:, :2 * sub] = both[c]
    keep[:, 2 * sub:] = gram
    give[:, :2 * sub] = both[1 - c]
    give[:, 2 * sub:] = gram


def solve_kernel(ids, *refs):
    if len(refs) == 3:
        (f0, f1, inverse), left, base = refs, None, None
    else:
        f0, f1, left, inverse, base = refs
    rank = inverse.shape[1]
    rows = f0.shape[0]
    start = f0.shape[1] - rank
    blocks = []
    for n in range(rank // 8):
        source, at = (f0, 8 * n) if 8 * n < rows else (f1, 8 * n - rows)
        blocks.append(source[at:at + 8, start:])
    lane = lax.broadcasted_iota(jnp.int32, (8, rank), 1)
    level = lax.broadcasted_iota(jnp.int32, (8, rank), 0)
    for j in range(rank):
        b, i = divmod(j, 8)
        at_lane = lane == j
        row = blocks[b][i:i + 1, :]
        scaled = jnp.where(at_lane[:1], 1.0, row) * (1.0 / row[:, j:j + 1])
        for n in range(b, rank // 8):
            column = blocks[n][:, j:j + 1]
            cleared = jnp.where(at_lane, 0.0, blocks[n]) - column * scaled
            blocks[n] = cleared if n > b else jnp.where(level > i, cleared, blocks[n])
    for n in range(rank // 8):
        here = level + 8 * n
        pivot = jnp.sum(jnp.where(lane == here, blocks[n], 0.0), axis=1, keepdims=True)
        unit = jnp.where(lane < here, blocks[n], jnp.where(lane == here, 1.0, 0.0))
        inverse[8 * n:8 * n + 8, :] = unit * lax.rsqrt(pivot)
    if left is not None:
        solved = mm(left[...], inverse[...], 1, 1, HIGHEST)
        base[...] = mm(solved, inverse[...], 1, 0, HIGHEST)


def final_kernel(chunks, first, ids, base, *refs):
    count = len(first)
    rights, merged, momentum = refs[:4 * count], refs[4 * count:4 * count + len(chunks)], refs[4 * count + len(chunks)]
    error_out, momentum_out, right = refs[-3:]
    step = pl.program_id(0)
    z, c = ids[1], ids[2]
    rows, width = rights[0].shape
    sub = width // 2
    s = step % 4

    for n in range(count):
        @pl.when(step == 4 * n)
        def _(n=n):
            own0, own1, other0, other1 = rights[4 * n:4 * n + 4]
            right[c, :rows] = own0[...]
            right[c, rows:] = own1[...]
            right[1 - c, :rows] = other0[...]
            right[1 - c, rows:] = other1[...]

    chunk = jnp.bitwise_xor(z, s)
    part = right[chunk // 2, :, pl.ds(pl.multiple_of((chunk % 2) * sub, sub), sub)]
    base_high, base_low = halves(base[...])
    part_high, part_low = halves(part)
    approx = mm(base_high, part_high, 1, 0) + mm(base_high, part_low, 1, 0) + mm(base_low, part_high, 1, 0)
    for t in range(4):
        @pl.when(s == t)
        def _(t=t):
            error_out[0] = merged[t][...] - approx

    momentum_out[...] = (MOMENTUM_RATE * momentum[...].astype(F32) + approx).astype(BF16)


def final(ids, base, rights, merged, momentum, carried, first):
    rows, inputs = momentum.shape
    sub = inputs // 16
    count = len(first)

    def other(step, ids):
        n = step // 4
        return jnp.bitwise_xor(ids[0], first[0] + n * (first[-1] - first[0]) // max(count - 1, 1))

    column = lambda step, ids: (0, jnp.bitwise_xor(ids[1], step % 4) * 4 + other(step, ids))
    column3 = lambda step, ids: (0,) + column(step, ids)
    still = lambda step, ids: (0, 0)
    flat = [x for blocks in rights for x in blocks]
    grid_spec = pltpu.PrefetchScalarGridSpec(
        num_scalar_prefetch=1,
        grid=(4 * count,),
        in_specs=[pl.BlockSpec(base.shape, still)]
        + [pl.BlockSpec(x.shape, still) for x in flat]
        + [
            pl.BlockSpec((rows, sub), lambda step, ids, at=at: (0, 4 * at + other(step, ids)))
            for _, at in merged
        ]
        + [pl.BlockSpec((rows, sub), column)]
        + [pl.BlockSpec(memory_space=pl.ANY)] * len(carried),
        out_specs=[pl.BlockSpec((1, rows, sub), column3), pl.BlockSpec((rows, sub), column)],
        scratch_shapes=[pltpu.VMEM((2, 2 * flat[0].shape[0], flat[0].shape[1]), F32)],
    )
    alias = 2 + len(flat) + 5
    return pl.pallas_call(
        lambda *refs: final_kernel(merged, first, *refs),
        grid_spec=grid_spec,
        out_shape=[jax.ShapeDtypeStruct((1, rows, inputs), F32), jax.ShapeDtypeStruct((rows, inputs), BF16)],
        input_output_aliases={alias + n: n for n in range(len(carried))},
        cost_estimate=pl.CostEstimate(
            flops=8 * rows * rows * sub * count, bytes_accessed=rows * sub * 48 * count, transcendentals=0
        ),
        compiler_params=params(),
        name="final",
    )(ids, base, *flat, *[array for array, _ in merged], momentum, *carried)


def own_right_kernel(ids, inverse, *refs):
    blocks, out = refs[:-1], refs[-1]
    r, z, c = ids[0], ids[1], ids[2]
    rows, width = blocks[0].shape
    sub = width // 2
    offset = pl.multiple_of((z % 2) * sub, sub)
    for n in range(2):
        need = jnp.bitwise_xor(2 * c + n, r)
        for k in range(4):
            for side in range(2):
                @pl.when((need == k) & ((z // 2 == c) == (side == 0)))
                def _(k=k, side=side, n=n):
                    top = blocks[4 * k + 2 * side][:, pl.ds(offset, sub)]
                    low = blocks[4 * k + 2 * side + 1][:, pl.ds(offset, sub)]
                    piece = jnp.concatenate([top, low], axis=0)
                    out[n * sub:(n + 1) * sub, :] = mm(piece, inverse[...], 0, 1, HIGHEST)


def per_device_square(x_mask, y_mask, a_mask, b_mask, grad_out, activations, error_feedback, momentum, right_factor):
    replicas = lax.axis_size("dp")
    me_dp, me_row = lax.axis_index("dp"), lax.axis_index("rows")
    ids = jnp.stack([me_dp, me_row // 2, me_row % 2]).astype(jnp.int32)
    rank = right_factor.shape[1]
    rows = grad_out.shape[1]
    block = activations.shape[1]
    sub = 2 * block // replicas
    over_x = lambda v: swap(v, "dp", x_mask)
    over_y = lambda v: swap(v, "dp", y_mask)
    over_a = lambda v: swap(v, "rows", a_mask)
    over_b = lambda v: swap(v, "rows", b_mask)
    over_c = lambda v: swap(v, "rows", 1)

    half_tokens = activations.shape[0] // 2
    grad_t = grad_out.T
    act = {0: activations, 1: over_a(activations), 3: over_b(activations)}

    other = over_c(right_factor)
    mine = jnp.where(me_dp // 2 == me_row % 2, right_factor, other)
    mine = lax.dynamic_slice_in_dim(mine, (me_dp % 2) * sub, sub, 0)

    merged, means = {}, {}

    def reduce_stage(chunks):
        acts = [part for s in chunks for part in (act[s], over_c(act[s]))]
        array, mx, my = stage(ids, grad_t, acts, error_feedback, chunks, sub)
        for n, s in enumerate(chunks):
            merged[s] = (array, n)
        return array, over_x(mx), over_y(my)

    def finish(chunks, array, rx, ry):
        ny, nx = second(ids, rx, ry, array, sub, len(chunks))
        outs = third(ids, rx, ry, over_y(ny), over_x(nx), array, sub, len(chunks), 1.0 / replicas)
        for n, s in enumerate(chunks):
            means[s] = outs[2 * n:2 * n + 2]

    stage_0 = reduce_stage((0,))
    held = lax.optimization_barrier((stage_0[0], act[1], act[3], mine))
    stage_0, act[1], act[3], mine = (held[0],) + stage_0[1:], held[1], held[2], held[3]
    merged[0] = (stage_0[0], 0)
    act[2] = jnp.concatenate([over_b(act[1][:half_tokens]), over_a(act[3][half_tokens:])], axis=0)
    stage_13 = reduce_stage((1, 3))
    finish((0,), *stage_0)
    stage_2 = reduce_stage((2,))
    finish((1, 3), *stage_13)
    finish((2,), *stage_2)
    rights = {0: mine, 1: over_a(mine), 3: over_b(mine)}
    rights[2] = over_b(rights[1])

    flat = [part for s in range(4) for part in means[s]]
    shape = lambda *dims: jax.ShapeDtypeStruct(dims, F32)
    left_flops = 6 * rows * 4 * sub * rank

    inverse, base = None, None
    for pass_index in range(PASSES):
        outs = [shape(rows // 2, rank)] * 2
        if pass_index == 0:
            p0, p1 = plain_call(first_left_kernel, outs, ids, flat + [rights[s] for s in range(4)], "left", left_flops)
        else:
            p0, p1 = plain_call(
                next_left_kernel, outs, ids, flat + [f0, f1, over_c(f0), over_c(f1)], "left", left_flops,
                [pltpu.VMEM((2, rank, 2 * sub), F32)],
            )
        p0, p1 = p0 + over_x(p0), p1 + over_y(p1)
        operands = flat + [p0, over_y(p0), p1, over_x(p1)]
        if pass_index:
            operands.append(inverse)
        left, keep, give = plain_call(
            lambda *refs, solved=pass_index > 0: right_kernel(solved, *refs),
            [shape(rows, rank), shape(rank, 2 * sub + rank), shape(rank, 2 * sub + rank)],
            ids, operands, "right", left_flops, [pltpu.VMEM((2, rank, 2 * sub), F32)],
        )
        total = keep + over_c(give)
        f0, f1 = total[:rank // 2], total[rank // 2:]
        f0, f1 = f0 + over_a(f0), f1 + over_b(f1)
        f0, f1 = f0 + over_b(f0), f1 + over_a(f1)
        if pass_index + 1 < PASSES:
            inverse = plain_call(solve_kernel, [shape(rank, rank)], ids, [f0, f1], "solve", 8 * left_flops)[0]
        else:
            inverse, base = plain_call(
                solve_kernel, [shape(rank, rank), shape(rows, rank)], ids, [f0, f1, left], "solve", 8 * left_flops
            )

    g0, g1 = f0[:, :2 * sub], f1[:, :2 * sub]
    x0, y1 = over_x(g0), over_y(g1)
    pieces = {0: (g0, g1), 1: (x0, over_x(g1)), 2: (over_y(g0), y1), 3: (over_y(x0), over_x(y1))}
    every = {k: [own0, own1, over_c(own0), over_c(own1)] for k, (own0, own1) in pieces.items()}
    sources = [merged[s] for s in range(4)]
    carried = final(ids, base, [every[k] for k in range(3)], sources, momentum, [], (0, 1, 2))
    carried = final(ids, base, [every[3]], sources, momentum, carried, (3,))
    own_rows = plain_call(
        own_right_kernel, [shape(rows, rank)], ids, [inverse] + [x for k in range(4) for x in every[k]],
        "own_right", 2 * rows * rank * rank * 6,
    )[0]
    return carried[0], carried[1], own_rows


def solution(mesh):
    replicas, row_blocks = mesh.shape["dp"], mesh.shape["rows"]
    side = 1 << ((replicas.bit_length() - 1) // 2)
    dp_masks = ring_masks(side) + [m * side for m in ring_masks(replicas // side)]
    chip_masks = [2 * m for m in ring_masks(row_blocks // 2)]

    square = len(dp_masks) == 2 and len(chip_masks) == 2

    def body(*args):
        sub = 2 * args[1].shape[1] // replicas
        if square and sub % 128 == 0 and args[4].shape[1] % 128 == 0:
            return per_device_square(*dp_masks, *chip_masks, *args)
        return per_device(dp_masks, chip_masks, *args)

    return jax.shard_map(
        body,
        mesh=mesh,
        in_specs=(
            P("dp", "rows"),
            P("dp", "rows"),
            P("dp", "rows", None),
            P("rows", None),
            P("rows", None),
        ),
        out_specs=(P("dp", "rows", None), P("rows", None), P("rows", None)),
        check_vma=False,
    )
```
